256 devices in a mesh: dom: 128 (over x, y, z), feat: 2 (over core).
Axes of the slice: x: 4, y: 4, z: 8, core: 2. Of those that a mesh axis runs over, the one named last changes fastest.
Arguments:
- grad_out: bfloat16 [65536, 512], P('dom', 'feat'), may hold values from -6 to 6
- preact: bfloat16 [65536, 512], P('dom', 'feat'), may hold values from -6 to 6
- aggregated: bfloat16 [65536, 512], P('dom', 'feat'), may hold values from -6 to 6
- weight: bfloat16 [512, 512], P(None, 'feat'), may hold values from -0.1875 to 0.1875
- tiles: bfloat16 [8192, 128, 128], P('dom'), may hold values from -0.25 to 0.25
- in_block: int32 [8192], P('dom'), may hold values from 0 to 11
- out_block: int32 [8192], P('dom'), may hold values from 0 to 3
- tile_count: int32 [128], P('dom'), may hold values from 4 to 64, as said below
- send_rows: int32 [128, 128, 8], P('dom'), may hold values from 0 to 511
Outputs:
- adjoint: bfloat16 [65536, 512], P('dom', 'feat')
- grad_weight: float32 [512, 512], P(None, 'feat')
The draws below stay inside these ranges and needn't reach their ends.
Inputs may be any that keep to these rules, and one draw needn't show every extreme that they name: Partition d uses its first tile_count[d] tile slots; some partition uses all 64.
All inputs are finite; a program needn't handle non-finite values.
Results may differ from the reference program's by a relative error of at most 0.014.
Values may be sent and summed in bfloat16 or wider, within the bound.
No kernel may reach another device: no remote copies, remote signals or barrier semaphores. Data moves between devices by JAX's collectives and lax.ppermute only.
A program may use at most 64 MiB of HBM per device.

```python
import math
import jax
import jax.numpy as jnp
from jax import lax

F = 512
TILE = 128
ITERS = 3
LB = 4
R = 8
ROWS_DEV = 512
TILES_DEV = 64
GHOST_BLOCKS = 8
NODES = 65536
N_DOM = 128


def draw_tile_count(key, part):
    first_key, second_key, third_key = jax.random.split(key, 3)
    first_draw = jax.random.randint(first_key, (N_DOM,), 0, 16)
    second_draw = jax.random.randint(second_key, (N_DOM,), 0, 16)
    counts = TILES_DEV // 16 * (1 + jnp.minimum(first_draw, second_draw))
    busiest = jax.random.randint(third_key, (), 0, N_DOM)
    return jnp.where(jnp.arange(N_DOM) == busiest, TILES_DEV, counts).astype(jnp.int32)


def set_ends(result, own_key, smallest, top_value):
    shape = result.shape
    index_at = [jax.random.randint(jax.random.fold_in(own_key, axis), (), 0, shape[axis]) for axis in range(len(shape))]
    result = result.at[tuple(index_at)].set(smallest)
    longest = shape.index(max(shape))
    index_at[longest] = (index_at[longest] + 1) % shape[longest]
    return result.at[tuple(index_at)].set(top_value)


def shard_levels(own_key, dims, pieces, smallest, high):
    level = 1.0
    for dim, blocks in pieces:
        draws = jax.random.uniform(jax.random.fold_in(jax.random.fold_in(own_key, 6), dim), (blocks,), jnp.float32, smallest / len(pieces), high / len(pieces))
        level = level * jnp.repeat(jnp.exp(draws), dims[dim] // blocks).reshape((-1,) + (1,) * (len(dims) - 1 - dim))
    return level


def gaussian(rng, dims, scale, reach, cuts=(), held_as=jnp.bfloat16):
    drawn = jax.random.normal(rng, dims, jnp.float32) * scale
    if len(cuts) > 0:
        drawn = shard_levels(rng, dims, cuts, -0.22, 0.18) * drawn
    return jnp.clip(drawn, min=-reach, max=reach).astype(held_as)


def setup_inputs(seed: int = 0) -> dict:
    seeds = jax.random.split(jax.random.key(seed), 10)
    return {
        "grad_out": gaussian(seeds[0], (NODES, F), 1.0, 6.0, ((0, 128), (1, 2))),
        "preact": gaussian(seeds[1], (NODES, F), 1.5, 6.0, ((0, 128), (1, 2))),
        "aggregated": gaussian(seeds[2], (NODES, F), 1.0, 6.0, ((0, 128), (1, 2))),
        "weight": gaussian(seeds[3], (F, F), (2 * F) ** -0.5, 0.1875, ((1, 2),)),
        "tiles": gaussian(seeds[4], (N_DOM * TILES_DEV, TILE, TILE), (4 * TILE) ** -0.5, 0.25, ((0, 128),)),
        "in_block": set_ends(jax.random.randint(seeds[5], (N_DOM * TILES_DEV,), 0, LB + GHOST_BLOCKS), jax.random.fold_in(seeds[5], 1), 0, (LB + GHOST_BLOCKS) - 1).astype(jnp.int32),
        "out_block": set_ends(jax.random.randint(seeds[6], (N_DOM * TILES_DEV,), 0, LB), jax.random.fold_in(seeds[6], 1), 0, LB - 1).astype(jnp.int32),
        "tile_count": draw_tile_count(jax.random.fold_in(seeds[9], 71), 0),
        "send_rows": set_ends(jax.random.randint(seeds[8], (N_DOM, N_DOM, R), 0, ROWS_DEV), jax.random.fold_in(seeds[8], 1), 0, ROWS_DEV - 1).astype(jnp.int32),
    }


def reference(grad_out, preact, aggregated, weight, tiles, in_block, out_block, tile_count, send_rows):
    row_count = LB * TILE
    hyperbolic = jnp.tanh(preact.astype(jnp.float32))
    slope = 1.0 - hyperbolic * hyperbolic
    source = grad_out.astype(jnp.float32)
    offsets = jnp.arange(N_DOM, dtype=jnp.int32)[:, None, None] * row_count
    global_rows = (offsets + send_rows.astype(jnp.int32)).astype(jnp.int32)
    ghost_index = jnp.transpose(global_rows, (1, 0, 2)).reshape(N_DOM, N_DOM * R)
    tiles_split = tiles.reshape(N_DOM, TILES_DEV, TILE, TILE)
    inputs_split = in_block.reshape(N_DOM, TILES_DEV)
    outputs_split = out_block.reshape(N_DOM, TILES_DEV)
    parts_index = jnp.arange(N_DOM, dtype=jnp.int32)
    adjoint_state = source
    for iteration in range(ITERS):
        scaled = (slope * adjoint_state).astype(jnp.bfloat16)
        mixed = jnp.dot(scaled, weight.T, preferred_element_type=jnp.float32).astype(jnp.bfloat16)

        def one_part(operands):
            tile_part, input_part, output_part, count_part, ghost_part, part_index = operands
            local_rows = lax.dynamic_slice_in_dim(mixed, part_index * row_count, row_count, 0)
            extended = jnp.concatenate([local_rows, jnp.take(mixed, ghost_part, axis=0)], 0)
            extended = extended.reshape(-1, TILE, F)
            picked = jnp.take(extended, input_part, axis=0).astype(jnp.float32)
            product = jnp.einsum('tij,tjf->tif', tile_part.astype(jnp.float32), picked, precision=lax.Precision.HIGHEST)
            live_slots = (jnp.arange(TILES_DEV, dtype=jnp.int32) < count_part).astype(jnp.float32)
            product = product * live_slots[:, None, None]
            accum = jnp.zeros((LB, TILE, F), jnp.float32).at[output_part].add(product)
            return accum.reshape(row_count, F)
        summed = lax.map(one_part, (tiles_split, inputs_split, outputs_split, tile_count, ghost_index, parts_index))
        adjoint_state = summed.reshape(NODES, F) + source
    adjoint = adjoint_state.astype(jnp.bfloat16)
    pre_grad = (slope * adjoint_state).astype(jnp.bfloat16)
    grad_weight = jnp.dot(aggregated.T, pre_grad, preferred_element_type=jnp.float32)
    grad_weight = grad_weight * jnp.float32(1.0 / math.sqrt(NODES))
    return (adjoint, grad_weight)
```

```python
import math

import jax
import jax.numpy as jnp
from jax import lax
from jax.experimental import pallas as pl
from jax.experimental.pallas import tpu as pltpu
from jax.sharding import PartitionSpec as P

ITERS = 3
BF16 = jnp.bfloat16
F32 = jnp.float32
VMEM = pl.BlockSpec(memory_space=pltpu.VMEM)
SMEM = pl.BlockSpec(memory_space=pltpu.SMEM)
SWAP = ((0, 1), (1, 0))


def params(mib):
    return pltpu.CompilerParams(vmem_limit_bytes=mib << 20)


def dot(a, b, dims=((1,), (0,))):
    return lax.dot_general(a, b, (dims, ((), ())), preferred_element_type=F32)


def densify_kernel(count, inputs, outputs, tiles, dense, total):
    in_blocks = dense.shape[1] // tiles.shape[1]
    out_blocks = dense.shape[0] // tiles.shape[1]
    size = tiles.shape[1]
    total[...] = jnp.zeros_like(total)

    def step(slot, carry):
        place = outputs[slot] * in_blocks + inputs[slot]
        total[place] += tiles[slot].astype(F32)
        return carry

    lax.fori_loop(0, count[0], step, 0)
    for out in range(out_blocks):
        for inp in range(in_blocks):
            dense[out * size:(out + 1) * size, inp * size:(inp + 1) * size] = total[
                out * in_blocks + inp
            ].astype(BF16)


def densify(count, inputs, outputs, tiles, out_blocks, in_blocks):
    size = tiles.shape[1]
    return pl.pallas_call(
        densify_kernel,
        out_shape=jax.ShapeDtypeStruct((out_blocks * size, in_blocks * size), BF16),
        in_specs=[SMEM, SMEM, SMEM, VMEM],
        out_specs=VMEM,
        scratch_shapes=[pltpu.VMEM((out_blocks * in_blocks, size, size), F32)],
        compiler_params=params(16),
        cost_estimate=pl.CostEstimate(flops=1 << 22, bytes_accessed=4 << 20, transcendentals=0),
        name="densify",
    )(count, inputs, outputs, tiles)


def mix_kernel(own, other, own_w, other_w, pick, mixed, outgoing):
    value = dot(own[...], own_w[...], ((1,), (1,))) + dot(other[...], other_w[...], ((1,), (1,)))
    value = value.astype(BF16)
    mixed[...] = value
    outgoing[...] = dot(pick[...], value).astype(BF16)


def mix(own, other, own_w, other_w, pick):
    rows, cols = own.shape
    return pl.pallas_call(
        mix_kernel,
        out_shape=(
            jax.ShapeDtypeStruct((rows, cols), BF16),
            jax.ShapeDtypeStruct((pick.shape[0], cols), BF16),
        ),
        in_specs=[VMEM] * 5,
        out_specs=(VMEM, VMEM),
        compiler_params=params(16),
        name="mix",
    )(own, other, own_w, other_w, pick)


def sweep_kernel(dense, mixed, ghosts, slope, source, scaled):
    rows = mixed.shape[0]
    state = dot(dense[:, :rows], mixed[...]) + dot(dense[:, rows:], ghosts[...])
    state = state + source[...].astype(F32)
    scaled[...] = (slope[...] * state).astype(BF16)


def sweep(dense, mixed, ghosts, slope, source):
    return pl.pallas_call(
        sweep_kernel,
        out_shape=jax.ShapeDtypeStruct(mixed.shape, BF16),
        in_specs=[VMEM] * 5,
        out_specs=VMEM,
        compiler_params=params(16),
        name="sweep",
    )(dense, mixed, ghosts, slope, source)


def last_kernel(half, dense, mixed, ghosts, slope, source, own, other, adjoint, pieces):
    rows, cols = mixed.shape
    state = dot(dense[:, :rows], mixed[...]) + dot(dense[:, rows:], ghosts[...])
    state = state + source[...].astype(F32)
    adjoint[...] = state.astype(BF16)
    pre_grad = (slope[...] * state).astype(BF16)
    count = pieces.shape[0] // 2
    for features, place in ((own, half[0]), (other, 1 - half[0])):
        part = dot(features[...], pre_grad, ((0,), (0,))).astype(BF16)
        for group in range(cols // 8):
            for side in range(cols // 128):
                pieces[place * count + group * (cols // 128) + side] = part[
                    group * 8:group * 8 + 8, side * 128:side * 128 + 128
                ]


def last(half, dense, mixed, ghosts, slope, source, own, other):
    rows, cols = mixed.shape
    return pl.pallas_call(
        last_kernel,
        out_shape=(
            jax.ShapeDtypeStruct((rows, cols), BF16),
            jax.ShapeDtypeStruct((2 * cols * cols // 1024, 8, 128), BF16),
        ),
        in_specs=[SMEM] + [VMEM] * 7,
        out_specs=(VMEM, VMEM),
        compiler_params=params(24),
        name="last",
    )(half, dense, mixed, ghosts, slope, source, own, other)


def total_kernel(scale, terms, spread):
    value = jnp.sum(terms[...].astype(F32), axis=0) * scale
    spread[...] = jnp.broadcast_to(value.astype(BF16)[None], spread.shape)


def unpack_kernel(pieces, grad):
    sides = grad.shape[1] // 128
    for piece in range(pieces.shape[0]):
        group, side = divmod(piece, sides)
        grad[group * 8:group * 8 + 8, side * 128:side * 128 + 128] = pieces[piece].astype(F32)


def shards(grad_out, preact, aggregated, weight, tiles, in_block, out_block, tile_count, send_rows):
    rows, cols = grad_out.shape
    tile_size = tiles.shape[1]
    peers = lax.axis_size("dom")
    sent_rows = send_rows[0].reshape(-1)
    sent = sent_rows.shape[0]
    half = lax.axis_index("feat")
    own_w = lax.dynamic_slice_in_dim(weight, half * cols, cols, 0)
    away_w = lax.dynamic_slice_in_dim(weight, (1 - half) * cols, cols, 0)
    other_w = lax.ppermute(away_w, "feat", SWAP)
    pick = (sent_rows[:, None] == jnp.arange(rows, dtype=jnp.int32)[None, :]).astype(BF16)
    hyperbolic = jnp.tanh(preact.astype(F32))
    slope = 1.0 - hyperbolic * hyperbolic
    scaled = (slope * grad_out.astype(F32)).astype(BF16)
    dense = None
    for iteration in range(ITERS):
        other = lax.ppermute(scaled, "feat", SWAP)
        mixed, outgoing = mix(scaled, other, own_w, other_w, pick)
        ghosts = lax.all_to_all(
            outgoing.reshape(peers, sent // peers, cols), "dom", split_axis=0, concat_axis=0, tiled=True
        ).reshape(sent, cols)
        if dense is None:
            dense = densify(
                tile_count, in_block, out_block, tiles, rows // tile_size, (rows + sent) // tile_size
            )
        if iteration < ITERS - 1:
            scaled = sweep(dense, mixed, ghosts, slope, grad_out)
    other_agg = lax.ppermute(aggregated, "feat", SWAP)
    adjoint, pieces = last(
        half.reshape(1), dense, mixed, ghosts, slope, grad_out, aggregated, other_agg
    )
    terms = lax.all_to_all(pieces, "dom", split_axis=0, concat_axis=0, tiled=True)
    spread = pl.pallas_call(
        lambda *refs: total_kernel(1.0 / math.sqrt(peers * rows), *refs),
        out_shape=jax.ShapeDtypeStruct(pieces.shape, BF16),
        in_specs=[VMEM],
        out_specs=VMEM,
        compiler_params=params(16),
        name="total",
    )(terms)
    gathered = lax.all_to_all(spread, "dom", split_axis=0, concat_axis=0, tiled=True)
    grad_weight = pl.pallas_call(
        unpack_kernel,
        out_shape=jax.ShapeDtypeStruct((2 * cols, cols), F32),
        in_specs=[VMEM],
        out_specs=VMEM,
        compiler_params=params(16),
        name="unpack",
    )(gathered)
    return adjoint, grad_weight


def solution(mesh):
    placed = (
        P("dom", "feat"),
        P("dom", "feat"),
        P("dom", "feat"),
        P(None, "feat"),
        P("dom", None, None),
        P("dom"),
        P("dom"),
        P("dom"),
        P("dom", None, None),
    )
    return jax.shard_map(
        shards,
        mesh=mesh,
        in_specs=placed,
        out_specs=(P("dom", "feat"), P(None, "feat")),
        check_vma=False,
    )
```

```python
import math

import jax
import jax.numpy as jnp
from jax import lax
from jax.experimental import pallas as pl
from jax.experimental.pallas import tpu as pltpu
from jax.sharding import PartitionSpec as P

ITERS = 3
RING = 8
BF16 = jnp.bfloat16
F32 = jnp.float32
VMEM = pl.BlockSpec(memory_space=pltpu.VMEM)
SMEM = pl.BlockSpec(memory_space=pltpu.SMEM)
HBM = pl.BlockSpec(memory_space=pltpu.HBM)
SWAP = ((0, 1), (1, 0))


def params(mib):
    return pltpu.CompilerParams(vmem_limit_bytes=mib << 20)


def dot(a, b, dims=((1,), (0,))):
    return lax.dot_general(a, b, (dims, ((), ())), preferred_element_type=F32)


def densify_kernel(count, inputs, outputs, tiles, dense, total, here, sems):
    size = tiles.shape[1]
    in_blocks = dense.shape[1] // size
    out_blocks = dense.shape[0] // size
    runs = here.shape[0]
    run = here.shape[1]
    fetches = [
        pltpu.make_async_copy(tiles.at[pl.ds(part * run, run)], here.at[part], sems.at[part])
        for part in range(runs)
    ]
    for part in range(runs):

        @pl.when(part * run < count[0])
        def _():
            fetches[part].start()

    total[...] = jnp.zeros_like(total)
    for part in range(runs):

        @pl.when(part * run < count[0])
        def _():
            fetches[part].wait()

            def step(slot, carry):
                place = outputs[part * run + slot] * in_blocks + inputs[part * run + slot]
                total[place] += here[part, slot].astype(F32)
                return carry

            lax.fori_loop(0, jnp.minimum(count[0] - part * run, run), step, 0)

    for out in range(out_blocks):
        for inp in range(in_blocks):
            dense[out * size:(out + 1) * size, inp * size:(inp + 1) * size] = total[
                out * in_blocks + inp
            ].astype(BF16)


def densify(count, inputs, outputs, tiles, out_blocks, in_blocks):
    size = tiles.shape[1]
    runs = 8
    return pl.pallas_call(
        densify_kernel,
        out_shape=jax.ShapeDtypeStruct((out_blocks * size, in_blocks * size), BF16),
        in_specs=[SMEM, SMEM, SMEM, HBM],
        out_specs=VMEM,
        scratch_shapes=[
            pltpu.VMEM((out_blocks * in_blocks, size, size), F32),
            pltpu.VMEM((runs, tiles.shape[0] // runs, size, size), BF16),
            pltpu.SemaphoreType.DMA((runs,)),
        ],
        compiler_params=params(60),
        cost_estimate=pl.CostEstimate(flops=1 << 22, bytes_accessed=4 << 20, transcendentals=0),
        name="densify",
    )(count, inputs, outputs, tiles)


def mix_kernel(half, own, other, own_w, other_w, pick, mixed, outgoing):
    cols = own.shape[1]
    mine = pl.ds(pl.multiple_of(half[0] * cols, cols), cols)
    value = dot(own[...], own_w[mine, :], ((1,), (1,)))
    value = value + dot(other[...], other_w[mine, :], ((1,), (1,)))
    value = value.astype(BF16)
    mixed[...] = value
    outgoing[...] = dot(pick[...], value).astype(BF16)


def mix(half, own, other, own_w, other_w, pick):
    rows, cols = own.shape
    return pl.pallas_call(
        mix_kernel,
        out_shape=(
            jax.ShapeDtypeStruct((rows, cols), BF16),
            jax.ShapeDtypeStruct((pick.shape[0], cols), BF16),
        ),
        in_specs=[SMEM] + [VMEM] * 5,
        out_specs=(VMEM, VMEM),
        compiler_params=params(16),
        name="mix",
    )(half, own, other, own_w, other_w, pick)


def sweep_kernel(dense, mixed, ghosts, slope, source, scaled):
    rows = mixed.shape[0]
    state = dot(dense[:, :rows], mixed[...]) + dot(dense[:, rows:], ghosts[...])
    state = state + source[...].astype(F32)
    scaled[...] = (slope[...] * state).astype(BF16)


def sweep(dense, mixed, ghosts, slope, source):
    return pl.pallas_call(
        sweep_kernel,
        out_shape=jax.ShapeDtypeStruct(mixed.shape, BF16),
        in_specs=[VMEM] * 5,
        out_specs=VMEM,
        compiler_params=params(16),
        name="sweep",
    )(dense, mixed, ghosts, slope, source)


def last_kernel(
    half, dense, mixed, ghosts, slope, source, own, other, adjoint, pieces, own_here, other_here, sems
):
    rows, cols = mixed.shape
    fetches = [
        pltpu.make_async_copy(own, own_here, sems.at[0]),
        pltpu.make_async_copy(other, other_here, sems.at[1]),
    ]
    for fetch in fetches:
        fetch.start()
    state = dot(dense[:, :rows], mixed[...]) + dot(dense[:, rows:], ghosts[...])
    state = state + source[...].astype(F32)
    adjoint[...] = state.astype(BF16)
    pre_grad = (slope[...] * state).astype(BF16)
    count = pieces.shape[0] // 2
    sides = cols // 128
    for fetch, features, place in (
        (fetches[0], own_here, half[0]),
        (fetches[1], other_here, 1 - half[0]),
    ):
        fetch.wait()
        part = dot(features[...], pre_grad, ((0,), (0,))).astype(BF16)
        for group in range(cols // 8):
            for side in range(sides):
                pieces[place * count + group * sides + side] = part[
                    group * 8:group * 8 + 8, side * 128:side * 128 + 128
                ]


def last(half, dense, mixed, ghosts, slope, source, own, other):
    rows, cols = mixed.shape
    return pl.pallas_call(
        last_kernel,
        out_shape=(
            jax.ShapeDtypeStruct((rows, cols), BF16),
            jax.ShapeDtypeStruct((2 * cols * cols // 1024, 8, 128), BF16),
        ),
        in_specs=[SMEM] + [VMEM] * 5 + [HBM] * 2,
        out_specs=(VMEM, VMEM),
        scratch_shapes=[
            pltpu.VMEM(own.shape, BF16),
            pltpu.VMEM(own.shape, BF16),
            pltpu.SemaphoreType.DMA((2,)),
        ],
        compiler_params=params(24),
        name="last",
    )(half, dense, mixed, ghosts, slope, source, own, other)


def total_kernel(terms_count, scale, terms, spread):
    value = terms[0].astype(F32)
    for term in range(1, terms_count):
        value = value + terms[term].astype(F32)
    value = (value * scale).astype(BF16)
    for copy in range(spread.shape[0]):
        spread[copy] = value


def total(terms, terms_count, copies, scale):
    blocks = terms.shape[0] // terms_count
    out = pl.pallas_call(
        lambda *refs: total_kernel(terms_count, scale, *refs),
        out_shape=jax.ShapeDtypeStruct((copies, blocks) + terms.shape[1:], BF16),
        in_specs=[VMEM],
        out_specs=VMEM,
        compiler_params=params(16),
        name="total",
    )(terms.reshape((terms_count, blocks) + terms.shape[1:]))
    return out.reshape((copies * blocks,) + terms.shape[1:])


def unpack_kernel(pieces, grad):
    sides = grad.shape[1] // 128
    for piece in range(pieces.shape[0]):
        group, side = divmod(piece, sides)
        grad[group * 8:group * 8 + 8, side * 128:side * 128 + 128] = pieces[piece].astype(F32)


def shards(grad_out, preact, aggregated, weight, tiles, in_block, out_block, tile_count, send_rows):
    rows, cols = grad_out.shape
    tile_size = tiles.shape[1]
    peers = lax.axis_size("dom")
    sent_rows = send_rows[0].reshape(-1)
    sent = sent_rows.shape[0]
    half = lax.axis_index("feat")
    half = half.reshape(1)
    other_weight = lax.ppermute(weight, "feat", SWAP)
    other_agg = lax.ppermute(aggregated, "feat", SWAP)
    pick = (sent_rows[:, None] == jnp.arange(rows, dtype=jnp.int32)[None, :]).astype(BF16)
    hyperbolic = jnp.tanh(preact.astype(F32))
    slope = 1.0 - hyperbolic * hyperbolic
    scaled = (slope * grad_out.astype(F32)).astype(BF16)
    dense = densify(
        tile_count, in_block, out_block, tiles, rows // tile_size, (rows + sent) // tile_size
    )
    for iteration in range(ITERS):
        other = lax.ppermute(scaled, "feat", SWAP)
        mixed, outgoing = mix(half, scaled, other, weight, other_weight, pick)
        if iteration == 0:
            outgoing, dense, other_agg = lax.optimization_barrier((outgoing, dense, other_agg))
        ghosts = lax.all_to_all(
            outgoing.reshape(peers, sent // peers, cols), "dom", split_axis=0, concat_axis=0, tiled=True
        ).reshape(sent, cols)
        if iteration < ITERS - 1:
            scaled = sweep(dense, mixed, ghosts, slope, grad_out)
    adjoint, pieces = last(half, dense, mixed, ghosts, slope, grad_out, aggregated, other_agg)
    lines = peers // RING
    across = [[line * RING + place for line in range(lines)] for place in range(RING)]
    along = [[line * RING + place for place in range(RING)] for line in range(lines)]

    def exchange(blocks, groups):
        return lax.all_to_all(
            blocks, "dom", split_axis=0, concat_axis=0, tiled=True, axis_index_groups=groups
        )

    terms = total(exchange(pieces, across), lines, RING, 1.0)
    spread = total(exchange(terms, along), RING, lines, 1.0 / math.sqrt(peers * rows))
    gathered = exchange(spread, across)
    grad_weight = pl.pallas_call(
        unpack_kernel,
        out_shape=jax.ShapeDtypeStruct((2 * cols, cols), F32),
        in_specs=[VMEM],
        out_specs=VMEM,
        compiler_params=params(16),
        name="unpack",
    )(gathered)
    return adjoint, grad_weight


def solution(mesh):
    placed = (
        P("dom", "feat"),
        P("dom", "feat"),
        P("dom", "feat"),
        P(None, "feat"),
        P("dom", None, None),
        P("dom"),
        P("dom"),
        P("dom"),
        P("dom", None, None),
    )
    return jax.shard_map(
        shards,
        mesh=mesh,
        in_specs=placed,
        out_specs=(P("dom", "feat"), P(None, "feat")),
        check_vma=False,
    )
```

```python
import math

import jax
import jax.numpy as jnp
from jax import lax
from jax.experimental import pallas as pl
from jax.experimental.pallas import tpu as pltpu
from jax.sharding import PartitionSpec as P

ITERS = 3
RING = 8
BF16 = jnp.bfloat16
F32 = jnp.float32
VMEM = pl.BlockSpec(memory_space=pltpu.VMEM)
SMEM = pl.BlockSpec(memory_space=pltpu.SMEM)
SWAP = ((0, 1), (1, 0))


def params(mib):
    return pltpu.CompilerParams(vmem_limit_bytes=mib << 20)


def dot(a, b, dims=((1,), (0,))):
    return lax.dot_general(a, b, (dims, ((), ())), preferred_element_type=F32)


def mix_kernel(half, own, other, own_w, other_w, pick, mixed, outgoing):
    cols = own.shape[1]
    mine = pl.ds(pl.multiple_of(half[0] * cols, cols), cols)
    value = dot(own[...], own_w[mine, :], ((1,), (1,)))
    value = value + dot(other[...], other_w[mine, :], ((1,), (1,)))
    value = value.astype(BF16)
    mixed[...] = value
    outgoing[...] = dot(pick[...], value).astype(BF16)


def mix(half, own, other, own_w, other_w, pick):
    rows, cols = own.shape
    return pl.pallas_call(
        mix_kernel,
        out_shape=(
            jax.ShapeDtypeStruct((rows, cols), BF16),
            jax.ShapeDtypeStruct((pick.shape[0], cols), BF16),
        ),
        in_specs=[SMEM] + [VMEM] * 5,
        out_specs=(VMEM, VMEM),
        compiler_params=params(16),
        cost_estimate=pl.CostEstimate(
            flops=8 * rows * cols * (2 * cols + pick.shape[0]), bytes_accessed=5 << 19, transcendentals=0
        ),
        name="mix",
    )(half, own, other, own_w, other_w, pick)


def new_state(dense, mixed, ghosts, source):
    rows = mixed.shape[0]
    state = dot(dense[:, :rows], mixed[...]) + dot(dense[:, rows:], ghosts[...])
    return state + source[...].astype(F32)


def first_kernel(places, tiles, mixed, ghosts, slope, source, scaled, dense, total):
    size = tiles.shape[1]
    out_blocks = dense.shape[0] // size
    in_blocks = dense.shape[1] // size
    total[...] = jnp.zeros_like(total)

    def step(slot, carry):
        total[places[slot]] += tiles[slot].astype(F32)
        return carry

    lax.fori_loop(0, tiles.shape[0], step, 0)
    for out in range(out_blocks):
        for inp in range(in_blocks):
            dense[out * size:(out + 1) * size, inp * size:(inp + 1) * size] = total[
                out * in_blocks + inp
            ].astype(BF16)
    scaled[...] = (slope[...] * new_state(dense, mixed, ghosts, source)).astype(BF16)


def first(places, tiles, mixed, ghosts, slope, source):
    size = tiles.shape[1]
    rows = mixed.shape[0]
    across = rows + ghosts.shape[0]
    pairs = rows * across // (size * size)
    return pl.pallas_call(
        first_kernel,
        out_shape=(
            jax.ShapeDtypeStruct(mixed.shape, BF16),
            jax.ShapeDtypeStruct((rows, across), BF16),
        ),
        in_specs=[SMEM] + [VMEM] * 5,
        out_specs=(VMEM, VMEM),
        scratch_shapes=[pltpu.VMEM((pairs + 1, size, size), F32)],
        compiler_params=params(24),
        name="first",
    )(places, tiles, mixed, ghosts, slope, source)


def sweep_kernel(dense, mixed, ghosts, slope, source, scaled):
    scaled[...] = (slope[...] * new_state(dense, mixed, ghosts, source)).astype(BF16)


def sweep(dense, mixed, ghosts, slope, source):
    return pl.pallas_call(
        sweep_kernel,
        out_shape=jax.ShapeDtypeStruct(mixed.shape, BF16),
        in_specs=[VMEM] * 5,
        out_specs=VMEM,
        compiler_params=params(16),
        name="sweep",
    )(dense, mixed, ghosts, slope, source)


def last_kernel(half, dense, mixed, ghosts, slope, source, own, other, adjoint, pieces):
    cols = mixed.shape[1]
    state = new_state(dense, mixed, ghosts, source)
    adjoint[...] = state.astype(BF16)
    pre_grad = (slope[...] * state).astype(BF16)
    count = pieces.shape[0] // 2
    sides = cols // 128
    for features, place in ((own, half[0]), (other, 1 - half[0])):
        part = dot(features[...], pre_grad, ((0,), (0,))).astype(BF16)
        for group in range(cols // 8):
            for side in range(sides):
                pieces[place * count + group * sides + side] = part[
                    group * 8:group * 8 + 8, side * 128:side * 128 + 128
                ]


def last(half, dense, mixed, ghosts, slope, source, own, other):
    rows, cols = mixed.shape
    return pl.pallas_call(
        last_kernel,
        out_shape=(
            jax.ShapeDtypeStruct((rows, cols), BF16),
            jax.ShapeDtypeStruct((2 * cols * cols // 1024, 8, 128), BF16),
        ),
        in_specs=[SMEM] + [VMEM] * 7,
        out_specs=(VMEM, VMEM),
        compiler_params=params(24),
        name="last",
    )(half, dense, mixed, ghosts, slope, source, own, other)


def total_kernel(terms_count, scale, terms, spread):
    value = terms[0].astype(F32)
    for term in range(1, terms_count):
        value = value + terms[term].astype(F32)
    value = (value * scale).astype(BF16)
    for copy in range(spread.shape[0]):
        spread[copy] = value


def total(terms, terms_count, copies, scale):
    blocks = terms.shape[0] // terms_count
    out = pl.pallas_call(
        lambda *refs: total_kernel(terms_count, scale, *refs),
        out_shape=jax.ShapeDtypeStruct((copies, blocks) + terms.shape[1:], BF16),
        in_specs=[VMEM],
        out_specs=VMEM,
        compiler_params=params(16),
        name="total",
    )(terms.reshape((terms_count, blocks) + terms.shape[1:]))
    return out.reshape((copies * blocks,) + terms.shape[1:])


def unpack_kernel(pieces, grad):
    sides = grad.shape[1] // 128
    for piece in range(pieces.shape[0]):
        group, side = divmod(piece, sides)
        grad[group * 8:group * 8 + 8, side * 128:side * 128 + 128] = pieces[piece].astype(F32)


def shards(grad_out, preact, aggregated, weight, tiles, in_block, out_block, tile_count, send_rows):
    rows, cols = grad_out.shape
    peers = lax.axis_size("dom")
    sent_rows = send_rows[0].reshape(-1)
    sent = sent_rows.shape[0]
    half = lax.axis_index("feat")
    half = half.reshape(1)
    other_weight = lax.ppermute(weight, "feat", SWAP)
    other_agg = lax.ppermute(aggregated, "feat", SWAP)
    pick = (sent_rows[:, None] == jnp.arange(rows, dtype=jnp.int32)[None, :]).astype(BF16)
    hyperbolic = jnp.tanh(preact.astype(F32))
    slope = 1.0 - hyperbolic * hyperbolic
    scaled = (slope * grad_out.astype(F32)).astype(BF16)
    in_blocks = (rows + sent) // tiles.shape[1]
    pairs = rows // tiles.shape[1] * in_blocks
    slots = jnp.arange(tiles.shape[0], dtype=jnp.int32)
    places = jnp.where(slots < tile_count[0], out_block * in_blocks + in_block, pairs)
    for iteration in range(ITERS):
        other = lax.ppermute(scaled, "feat", SWAP)
        mixed, outgoing = mix(half, scaled, other, weight, other_weight, pick)
        if iteration == 0:
            outgoing, other_agg, places = lax.optimization_barrier((outgoing, other_agg, places))
        ghosts = lax.all_to_all(
            outgoing.reshape(peers, sent // peers, cols), "dom", split_axis=0, concat_axis=0, tiled=True
        ).reshape(sent, cols)
        if iteration == 0:
            scaled, dense = first(places, tiles, mixed, ghosts, slope, grad_out)
        elif iteration < ITERS - 1:
            scaled = sweep(dense, mixed, ghosts, slope, grad_out)
    adjoint, pieces = last(half, dense, mixed, ghosts, slope, grad_out, aggregated, other_agg)
    lines = peers // RING
    across = [[line * RING + place for line in range(lines)] for place in range(RING)]
    along = [[line * RING + place for place in range(RING)] for line in range(lines)]

    def exchange(blocks, groups):
        return lax.all_to_all(
            blocks, "dom", split_axis=0, concat_axis=0, tiled=True, axis_index_groups=groups
        )

    terms = total(exchange(pieces, across), lines, RING, 1.0)
    spread = total(exchange(terms, along), RING, lines, 1.0 / math.sqrt(peers * rows))
    gathered = exchange(spread, across)
    grad_weight = pl.pallas_call(
        unpack_kernel,
        out_shape=jax.ShapeDtypeStruct((2 * cols, cols), F32),
        in_specs=[VMEM],
        out_specs=VMEM,
        compiler_params=params(16),
        name="unpack",
    )(gathered)
    return adjoint, grad_weight


def solution(mesh):
    placed = (
        P("dom", "feat"),
        P("dom", "feat"),
        P("dom", "feat"),
        P(None, "feat"),
        P("dom", None, None),
        P("dom"),
        P("dom"),
        P("dom"),
        P("dom", None, None),
    )
    return jax.shard_map(
        shards,
        mesh=mesh,
        in_specs=placed,
        out_specs=(P("dom", "feat"), P(None, "feat")),
        check_vma=False,
    )
```

```python
import math

import jax
import jax.numpy as jnp
from jax import lax
from jax.experimental import pallas as pl
from jax.experimental.pallas import tpu as pltpu
from jax.sharding import PartitionSpec as P

ITERS = 3
RING = 8
BF16 = jnp.bfloat16
F32 = jnp.float32
VMEM = pl.BlockSpec(memory_space=pltpu.VMEM)
SMEM = pl.BlockSpec(memory_space=pltpu.SMEM)
PARTS = 4
SWAP = ((0, 1), (1, 0))


def params(mib):
    return pltpu.CompilerParams(vmem_limit_bytes=mib << 20)


def dot(a, b, dims=((1,), (0,))):
    return lax.dot_general(a, b, (dims, ((), ())), preferred_element_type=F32)


def mix_kernel(half, own, other, own_w, other_w, pick, mixed, outgoing):
    cols = own.shape[1]
    mine = pl.ds(pl.multiple_of(half[0] * cols, cols), cols)
    value = dot(own[...], own_w[mine, :], ((1,), (1,)))
    value = value + dot(other[...], other_w[mine, :], ((1,), (1,)))
    value = value.astype(BF16)
    mixed[...] = value
    outgoing[...] = dot(pick[...], value).astype(BF16)


def mix(half, own, other, own_w, other_w, pick):
    rows, cols = own.shape
    return pl.pallas_call(
        mix_kernel,
        out_shape=(
            jax.ShapeDtypeStruct((rows, cols), BF16),
            jax.ShapeDtypeStruct((pick.shape[0], cols), BF16),
        ),
        in_specs=[SMEM] + [VMEM] * 5,
        out_specs=(VMEM, VMEM),
        compiler_params=params(16),
        cost_estimate=pl.CostEstimate(
            flops=8 * rows * cols * (2 * cols + pick.shape[0]), bytes_accessed=5 << 19, transcendentals=0
        ),
        name="mix",
    )(half, own, other, own_w, other_w, pick)


def new_state(dense, mixed, ghosts, source):
    rows = mixed.shape[0]
    state = dot(dense[:, :rows], mixed[...]) + dot(dense[:, rows:], ghosts[...])
    return state + source[...].astype(F32)


def first_kernel(places, tiles, mixed, ghosts, slope, source, scaled, dense, total, seen):
    size = tiles.shape[1]
    out_blocks = dense.shape[0] // size
    in_blocks = dense.shape[1] // size
    for pair in range(total.shape[0]):
        seen[pair] = 0

    def step(slot, carry):
        place = places[slot]
        before = jnp.where(seen[place] == 1, total[place], 0.0)
        total[place] = before + tiles[slot].astype(F32)
        seen[place] = 1
        return carry

    lax.fori_loop(0, tiles.shape[0], step, 0, unroll=4)
    for out in range(out_blocks):
        for inp in range(in_blocks):
            pair = out * in_blocks + inp
            value = jnp.where(seen[pair] == 1, total[pair], 0.0)
            dense[out * size:(out + 1) * size, inp * size:(inp + 1) * size] = value.astype(BF16)
    scaled[...] = (slope[...] * new_state(dense, mixed, ghosts, source)).astype(BF16)


def first(places, tiles, mixed, ghosts, slope, source):
    size = tiles.shape[1]
    rows = mixed.shape[0]
    across = rows + ghosts.shape[0]
    pairs = rows * across // (size * size)
    return pl.pallas_call(
        first_kernel,
        out_shape=(
            jax.ShapeDtypeStruct(mixed.shape, BF16),
            jax.ShapeDtypeStruct((rows, across), BF16),
        ),
        in_specs=[SMEM] + [VMEM] * 5,
        out_specs=(VMEM, VMEM),
        scratch_shapes=[pltpu.VMEM((pairs + 1, size, size), F32), pltpu.SMEM((pairs + 1,), jnp.int32)],
        compiler_params=params(24),
        name="first",
    )(places, tiles, mixed, ghosts, slope, source)


def sweep_kernel(dense, mixed, ghosts, slope, source, scaled):
    scaled[...] = (slope[...] * new_state(dense, mixed, ghosts, source)).astype(BF16)


def sweep(dense, mixed, ghosts, slope, source):
    return pl.pallas_call(
        sweep_kernel,
        out_shape=jax.ShapeDtypeStruct(mixed.shape, BF16),
        in_specs=[VMEM] * 5,
        out_specs=VMEM,
        compiler_params=params(16),
        name="sweep",
    )(dense, mixed, ghosts, slope, source)


def last_kernel(
    half, dense, mixed, ghosts, slope, source, own, other, adjoint, pieces, rounded, sem
):
    cols = mixed.shape[1]
    state = new_state(dense, mixed, ghosts, source)
    rounded[...] = state.astype(BF16)
    leave = pltpu.make_async_copy(rounded, adjoint, sem)
    leave.start()
    pre_grad = (slope[...] * state).astype(BF16)
    count = pieces.shape[0] // 2
    sides = cols // 128
    for features, place in ((own, half[0]), (other, 1 - half[0])):
        part = dot(features[...], pre_grad, ((0,), (0,))).astype(BF16)
        for group in range(cols // 8):
            for side in range(sides):
                pieces[place * count + group * sides + side] = part[
                    group * 8:group * 8 + 8, side * 128:side * 128 + 128
                ]
    leave.wait()


def last(half, dense, mixed, ghosts, slope, source, own, other):
    rows, cols = mixed.shape
    return pl.pallas_call(
        last_kernel,
        out_shape=(
            jax.ShapeDtypeStruct((rows, cols), BF16),
            jax.ShapeDtypeStruct((2 * cols * cols // 1024, 8, 128), BF16),
        ),
        in_specs=[SMEM] + [VMEM] * 7,
        out_specs=(pl.BlockSpec(memory_space=pl.ANY), VMEM),
        scratch_shapes=[pltpu.VMEM((rows, cols), BF16), pltpu.SemaphoreType.DMA],
        compiler_params=params(24),
        name="last",
    )(half, dense, mixed, ghosts, slope, source, own, other)


def total_kernel(terms_count, scale, terms, spread):
    value = terms[0].astype(F32)
    for term in range(1, terms_count):
        value = value + terms[term].astype(F32)
    value = (value * scale).astype(BF16)
    for copy in range(spread.shape[0]):
        spread[copy] = value


def total(terms, terms_count, copies, scale):
    blocks = terms.shape[0] // terms_count
    out = pl.pallas_call(
        lambda *refs: total_kernel(terms_count, scale, *refs),
        out_shape=jax.ShapeDtypeStruct((copies, blocks) + terms.shape[1:], BF16),
        in_specs=[VMEM],
        out_specs=VMEM,
        compiler_params=params(16),
        name="total",
    )(terms.reshape((terms_count, blocks) + terms.shape[1:]))
    return out.reshape((copies * blocks,) + terms.shape[1:])


def unpack_kernel(pieces, grad):
    sides = grad.shape[1] // 128
    for piece in range(pieces.shape[0]):
        group, side = divmod(piece, sides)
        grad[group * 8:group * 8 + 8, side * 128:side * 128 + 128] = pieces[piece].astype(F32)


def shards(grad_out, preact, aggregated, weight, tiles, in_block, out_block, tile_count, send_rows):
    rows, cols = grad_out.shape
    peers = lax.axis_size("dom")
    sent_rows = send_rows[0].reshape(-1)
    sent = sent_rows.shape[0]
    half = lax.axis_index("feat")
    half = half.reshape(1)
    other_weight = lax.ppermute(weight, "feat", SWAP)
    pick = (sent_rows[:, None] == jnp.arange(rows, dtype=jnp.int32)[None, :]).astype(BF16)
    hyperbolic = jnp.tanh(preact.astype(F32))
    slope = 1.0 - hyperbolic * hyperbolic
    scaled = (slope * grad_out.astype(F32)).astype(BF16)
    in_blocks = (rows + sent) // tiles.shape[1]
    pairs = rows // tiles.shape[1] * in_blocks
    slots = jnp.arange(tiles.shape[0], dtype=jnp.int32)
    places = jnp.where(slots < tile_count[0], out_block * in_blocks + in_block, pairs)
    for iteration in range(ITERS):
        other = lax.ppermute(scaled, "feat", SWAP)
        mixed, outgoing = mix(half, scaled, other, weight, other_weight, pick)
        if iteration == 0:
            outgoing, places = lax.optimization_barrier((outgoing, places))
        if iteration == 1:
            outgoing, other_agg = lax.optimization_barrier((outgoing, other_agg))
        ghosts = lax.all_to_all(
            outgoing.reshape(peers, sent // peers, cols), "dom", split_axis=0, concat_axis=0, tiled=True
        ).reshape(sent, cols)
        if iteration == 0:
            scaled, dense = first(places, tiles, mixed, ghosts, slope, grad_out)
            scaled, aggregated = lax.optimization_barrier((scaled, aggregated))
            other_agg = lax.ppermute(aggregated, "feat", SWAP)
        elif iteration < ITERS - 1:
            scaled = sweep(dense, mixed, ghosts, slope, grad_out)
    adjoint, pieces = last(half, dense, mixed, ghosts, slope, grad_out, aggregated, other_agg)
    lines = peers // RING
    across = [[line * RING + place for line in range(lines)] for place in range(RING)]
    along = [[line * RING + place for place in range(RING)] for line in range(lines)]

    def exchange(blocks, groups):
        return lax.all_to_all(
            blocks, "dom", split_axis=0, concat_axis=0, tiled=True, axis_index_groups=groups
        )

    terms = total(exchange(pieces, across), lines, RING, 1.0)
    spread = total(exchange(terms, along), RING, lines, 1.0 / math.sqrt(peers * rows))
    gathered = exchange(spread, across)
    grad_weight = pl.pallas_call(
        unpack_kernel,
        out_shape=jax.ShapeDtypeStruct((2 * cols, cols), F32),
        grid=(PARTS,),
        in_specs=[pl.BlockSpec((gathered.shape[0] // PARTS, 8, 128), lambda part: (part, 0, 0))],
        out_specs=pl.BlockSpec((2 * cols // PARTS, cols), lambda part: (part, 0)),
        compiler_params=params(16),
        name="unpack",
    )(gathered)
    return adjoint, grad_weight


def solution(mesh):
    placed = (
        P("dom", "feat"),
        P("dom", "feat"),
        P("dom", "feat"),
        P(None, "feat"),
        P("dom", None, None),
        P("dom"),
        P("dom"),
        P("dom"),
        P("dom", None, None),
    )
    return jax.shard_map(
        shards,
        mesh=mesh,
        in_specs=placed,
        out_specs=(P("dom", "feat"), P(None, "feat")),
        check_vma=False,
    )
```

```python
import math

import jax
import jax.numpy as jnp
from jax import lax
from jax.experimental import pallas as pl
from jax.experimental.pallas import tpu as pltpu
from jax.sharding import PartitionSpec as P

ITERS = 3
RING = 8
BF16 = jnp.bfloat16
F32 = jnp.float32
VMEM = pl.BlockSpec(memory_space=pltpu.VMEM)
SMEM = pl.BlockSpec(memory_space=pltpu.SMEM)
SWAP = ((0, 1), (1, 0))


def params(mib):
    return pltpu.CompilerParams(vmem_limit_bytes=mib << 20)


def dot(a, b, dims=((1,), (0,))):
    return lax.dot_general(a, b, (dims, ((), ())), preferred_element_type=F32)


def choose_kernel(wanted, pick):
    step, rows = 2 * wanted.shape[0], pick.shape[1]
    row = lax.broadcasted_iota(jnp.int32, (wanted.shape[0], rows), 1)
    for pair in range(wanted.shape[1] // 2):
        parts = [
            (wanted[:, peer:peer + 1] == row).astype(F32) for peer in (2 * pair, 2 * pair + 1)
        ]
        pick[pair * step:pair * step + step, :] = jnp.concatenate(parts, axis=0).astype(BF16)


def choose(wanted, rows):
    return pl.pallas_call(
        choose_kernel,
        out_shape=jax.ShapeDtypeStruct((wanted.shape[0] * wanted.shape[1], rows), BF16),
        in_specs=[VMEM],
        out_specs=VMEM,
        compiler_params=params(16),
        name="choose",
    )(wanted)


def mix_kernel(half, count, own, other, own_w, other_w, pick, mixed, outgoing):
    cols = own.shape[1]
    mine = pl.ds(pl.multiple_of(half[0] * cols, cols), cols)
    value = dot(own[...], own_w[mine, :], ((1,), (1,)))
    value = value + dot(other[...], other_w[mine, :], ((1,), (1,)))
    value = value.astype(BF16)
    mixed[...] = value
    outgoing[...] = dot(pick[...], value).astype(BF16)


def mix(half, count, own, other, own_w, other_w, pick):
    rows, cols = own.shape
    return pl.pallas_call(
        mix_kernel,
        out_shape=(
            jax.ShapeDtypeStruct((rows, cols), BF16),
            jax.ShapeDtypeStruct((pick.shape[0], cols), BF16),
        ),
        in_specs=[SMEM] * 2 + [VMEM] * 5,
        out_specs=(VMEM, VMEM),
        compiler_params=params(16),
        cost_estimate=pl.CostEstimate(
            flops=8 * rows * cols * (2 * cols + pick.shape[0]), bytes_accessed=5 << 19, transcendentals=0
        ),
        name="mix",
    )(half, count, own, other, own_w, other_w, pick)


def new_state(dense, mixed, ghosts, source):
    rows = mixed.shape[0]
    state = dot(dense[:, :rows], mixed[...]) + dot(dense[:, rows:], ghosts[...])
    return state + source[...].astype(F32)


def first_kernel(
    count, inputs, outputs, tiles, mixed, ghosts, slope, source, scaled, dense, total
):
    size = tiles.shape[1]
    out_blocks = dense.shape[0] // size
    in_blocks = dense.shape[1] // size
    total[...] = jnp.zeros_like(total)

    def step(slot, carry):
        total[outputs[slot] * in_blocks + inputs[slot]] += tiles[slot].astype(F32)
        return carry

    lax.fori_loop(0, count[0], step, 0)
    for out in range(out_blocks):
        for inp in range(in_blocks):
            dense[out * size:(out + 1) * size, inp * size:(inp + 1) * size] = total[
                out * in_blocks + inp
            ].astype(BF16)
    scaled[...] = (slope[...] * new_state(dense, mixed, ghosts, source)).astype(BF16)


def first(count, inputs, outputs, tiles, mixed, ghosts, slope, source):
    size = tiles.shape[1]
    rows = mixed.shape[0]
    across = rows + ghosts.shape[0]
    pairs = rows * across // (size * size)
    return pl.pallas_call(
        first_kernel,
        out_shape=(
            jax.ShapeDtypeStruct(mixed.shape, BF16),
            jax.ShapeDtypeStruct((rows, across), BF16),
        ),
        in_specs=[SMEM] * 3 + [VMEM] * 5,
        out_specs=(VMEM, VMEM),
        scratch_shapes=[pltpu.VMEM((pairs, size, size), F32)],
        compiler_params=params(24),
        name="first",
    )(count, inputs, outputs, tiles, mixed, ghosts, slope, source)


def sweep_kernel(dense, mixed, ghosts, slope, source, scaled):
    scaled[...] = (slope[...] * new_state(dense, mixed, ghosts, source)).astype(BF16)


def sweep(dense, mixed, ghosts, slope, source):
    return pl.pallas_call(
        sweep_kernel,
        out_shape=jax.ShapeDtypeStruct(mixed.shape, BF16),
        in_specs=[VMEM] * 5,
        out_specs=VMEM,
        compiler_params=params(16),
        name="sweep",
    )(dense, mixed, ghosts, slope, source)


def last_kernel(half, dense, mixed, ghosts, slope, source, own, other, adjoint, pieces):
    cols = mixed.shape[1]
    state = new_state(dense, mixed, ghosts, source)
    adjoint[...] = state.astype(BF16)
    pre_grad = (slope[...] * state).astype(BF16)
    count = pieces.shape[0] // 2
    sides = cols // 128
    for features, place in ((own, half[0]), (other, 1 - half[0])):
        part = dot(features[...], pre_grad, ((0,), (0,))).astype(BF16)
        for group in range(cols // 8):
            for side in range(sides):
                pieces[place * count + group * sides + side] = part[
                    group * 8:group * 8 + 8, side * 128:side * 128 + 128
                ]


def last(half, dense, mixed, ghosts, slope, source, own, other):
    rows, cols = mixed.shape
    return pl.pallas_call(
        last_kernel,
        out_shape=(
            jax.ShapeDtypeStruct((rows, cols), BF16),
            jax.ShapeDtypeStruct((2 * cols * cols // 1024, 8, 128), BF16),
        ),
        in_specs=[SMEM] + [VMEM] * 7,
        out_specs=(VMEM, VMEM),
        compiler_params=params(24),
        name="last",
    )(half, dense, mixed, ghosts, slope, source, own, other)


def total_kernel(terms_count, scale, terms, spread):
    value = terms[0].astype(F32)
    for term in range(1, terms_count):
        value = value + terms[term].astype(F32)
    value = (value * scale).astype(BF16)
    for copy in range(spread.shape[0]):
        spread[copy] = value


def total(terms, terms_count, copies, scale):
    blocks = terms.shape[0] // terms_count
    out = pl.pallas_call(
        lambda *refs: total_kernel(terms_count, scale, *refs),
        out_shape=jax.ShapeDtypeStruct((copies, blocks) + terms.shape[1:], BF16),
        in_specs=[VMEM],
        out_specs=VMEM,
        compiler_params=params(16),
        name="total",
    )(terms.reshape((terms_count, blocks) + terms.shape[1:]))
    return out.reshape((copies * blocks,) + terms.shape[1:])


def unpack_kernel(pieces, grad):
    sides = grad.shape[1] // 128
    for piece in range(pieces.shape[0]):
        group, side = divmod(piece, sides)
        grad[group * 8:group * 8 + 8, side * 128:side * 128 + 128] = pieces[piece].astype(F32)


def shards(grad_out, preact, aggregated, weight, tiles, in_block, out_block, tile_count, send_rows):
    rows, cols = grad_out.shape
    peers = lax.axis_size("dom")
    sent = send_rows.shape[1] * send_rows.shape[2]
    half = lax.axis_index("feat")
    half = half.reshape(1)
    other_weight = lax.ppermute(weight, "feat", SWAP)
    pick = choose(send_rows[0].T, rows)
    hyperbolic = jnp.tanh(preact.astype(F32))
    slope = 1.0 - hyperbolic * hyperbolic
    scaled = (slope * grad_out.astype(F32)).astype(BF16)
    for iteration in range(ITERS):
        other = lax.ppermute(scaled, "feat", SWAP)
        mixed, outgoing = mix(half, tile_count, scaled, other, weight, other_weight, pick)
        if iteration == 1:
            outgoing, other_agg = lax.optimization_barrier((outgoing, other_agg))
        ghosts = lax.all_to_all(
            outgoing.reshape(peers, sent // peers, cols), "dom", split_axis=0, concat_axis=0, tiled=True
        ).reshape(sent, cols)
        if iteration == 0:
            scaled, dense = first(
                tile_count, in_block, out_block, tiles, mixed, ghosts, slope, grad_out
            )
            scaled, aggregated = lax.optimization_barrier((scaled, aggregated))
            other_agg = lax.ppermute(aggregated, "feat", SWAP)
        elif iteration < ITERS - 1:
            scaled = sweep(dense, mixed, ghosts, slope, grad_out)
    adjoint, pieces = last(half, dense, mixed, ghosts, slope, grad_out, aggregated, other_agg)
    lines = peers // RING
    across = [[line * RING + place for line in range(lines)] for place in range(RING)]
    along = [[line * RING + place for place in range(RING)] for line in range(lines)]

    def exchange(blocks, groups):
        return lax.all_to_all(
            blocks, "dom", split_axis=0, concat_axis=0, tiled=True, axis_index_groups=groups
        )

    terms = total(exchange(pieces, across), lines, RING, 1.0)
    spread = total(exchange(terms, along), RING, lines, 1.0 / math.sqrt(peers * rows))
    gathered = exchange(spread, across)
    grad_weight = pl.pallas_call(
        unpack_kernel,
        out_shape=jax.ShapeDtypeStruct((2 * cols, cols), F32),
        in_specs=[VMEM],
        out_specs=VMEM,
        compiler_params=params(16),
        name="unpack",
    )(gathered)
    return adjoint, grad_weight


def solution(mesh):
    placed = (
        P("dom", "feat"),
        P("dom", "feat"),
        P("dom", "feat"),
        P(None, "feat"),
        P("dom", None, None),
        P("dom"),
        P("dom"),
        P("dom"),
        P("dom", None, None),
    )
    return jax.shard_map(
        shards,
        mesh=mesh,
        in_specs=placed,
        out_specs=(P("dom", "feat"), P(None, "feat")),
        check_vma=False,
    )
```

```python
import math

import jax
import jax.numpy as jnp
from jax import lax
from jax.experimental import pallas as pl
from jax.experimental.pallas import tpu as pltpu
from jax.sharding import PartitionSpec as P

ITERS = 3
RING = 8
BF16 = jnp.bfloat16
F32 = jnp.float32
VMEM = pl.BlockSpec(memory_space=pltpu.VMEM)
SMEM = pl.BlockSpec(memory_space=pltpu.SMEM)
SWAP = ((0, 1), (1, 0))


def params(mib):
    return pltpu.CompilerParams(vmem_limit_bytes=mib << 20)


def dot(a, b, dims=((1,), (0,))):
    return lax.dot_general(a, b, (dims, ((), ())), preferred_element_type=F32)


def split(size):
    return slice(0, size // 2), slice(size // 2, size)


def choose_kernel(wanted, pick):
    step, rows = 2 * wanted.shape[0], pick.shape[1]
    row = lax.broadcasted_iota(jnp.int32, (wanted.shape[0], rows), 1)
    for pair in range(wanted.shape[1] // 2):
        parts = [
            (wanted[:, peer:peer + 1] == row).astype(F32) for peer in (2 * pair, 2 * pair + 1)
        ]
        pick[pair * step:pair * step + step, :] = jnp.concatenate(parts, axis=0).astype(BF16)


def choose(wanted, rows):
    return pl.pallas_call(
        choose_kernel,
        out_shape=jax.ShapeDtypeStruct((wanted.shape[0] * wanted.shape[1], rows), BF16),
        in_specs=[VMEM],
        out_specs=VMEM,
        compiler_params=params(16),
        name="choose",
    )(wanted)


def mix_kernel(half, count, own, other, own_w, other_w, pick, mixed, outgoing):
    cols = own.shape[1]
    mine = pl.ds(pl.multiple_of(half[0] * cols, cols), cols)
    ends = []
    for part in split(own.shape[0]):
        value = dot(own[part, :], own_w[mine, :], ((1,), (1,)))
        value = value + dot(other[part, :], other_w[mine, :], ((1,), (1,)))
        ends.append(value.astype(BF16))
        mixed[part, :] = ends[-1]
    value = jnp.concatenate(ends, axis=0)
    for part in split(pick.shape[0]):
        outgoing[part, :] = dot(pick[part, :], value).astype(BF16)


def mix(half, count, own, other, own_w, other_w, pick):
    rows, cols = own.shape
    return pl.pallas_call(
        mix_kernel,
        out_shape=(
            jax.ShapeDtypeStruct((rows, cols), BF16),
            jax.ShapeDtypeStruct((pick.shape[0], cols), BF16),
        ),
        in_specs=[SMEM] * 2 + [VMEM] * 5,
        out_specs=(VMEM, VMEM),
        compiler_params=params(16),
        cost_estimate=pl.CostEstimate(
            flops=8 * rows * cols * (2 * cols + pick.shape[0]), bytes_accessed=5 << 19, transcendentals=0
        ),
        name="mix",
    )(half, count, own, other, own_w, other_w, pick)


def new_state(dense, mixed, ghosts, source):
    rows = mixed.shape[0]
    state = dot(dense[:, :rows], mixed[...]) + dot(dense[:, rows:], ghosts[...])
    return state + source[...].astype(F32)


def first_kernel(
    count, inputs, outputs, tiles, mixed, ghosts, slope, source, scaled, dense, total
):
    size = tiles.shape[1]
    out_blocks = dense.shape[0] // size
    in_blocks = dense.shape[1] // size
    total[...] = jnp.zeros_like(total)

    def step(slot, carry):
        total[outputs[slot] * in_blocks + inputs[slot]] += tiles[slot].astype(F32)
        return carry

    lax.fori_loop(0, count[0], step, 0)
    for out in range(out_blocks):
        for inp in range(in_blocks):
            dense[out * size:(out + 1) * size, inp * size:(inp + 1) * size] = total[
                out * in_blocks + inp
            ].astype(BF16)
    scaled[...] = (slope[...] * new_state(dense, mixed, ghosts, source)).astype(BF16)


def first(count, inputs, outputs, tiles, mixed, ghosts, slope, source):
    size = tiles.shape[1]
    rows = mixed.shape[0]
    across = rows + ghosts.shape[0]
    pairs = rows * across // (size * size)
    return pl.pallas_call(
        first_kernel,
        out_shape=(
            jax.ShapeDtypeStruct(mixed.shape, BF16),
            jax.ShapeDtypeStruct((rows, across), BF16),
        ),
        in_specs=[SMEM] * 3 + [VMEM] * 5,
        out_specs=(VMEM, VMEM),
        scratch_shapes=[pltpu.VMEM((pairs, size, size), F32)],
        compiler_params=params(24),
        name="first",
    )(count, inputs, outputs, tiles, mixed, ghosts, slope, source)


def sweep_kernel(dense, mixed, ghosts, slope, source, scaled):
    scaled[...] = (slope[...] * new_state(dense, mixed, ghosts, source)).astype(BF16)


def sweep(dense, mixed, ghosts, slope, source):
    return pl.pallas_call(
        sweep_kernel,
        out_shape=jax.ShapeDtypeStruct(mixed.shape, BF16),
        in_specs=[VMEM] * 5,
        out_specs=VMEM,
        compiler_params=params(16),
        name="sweep",
    )(dense, mixed, ghosts, slope, source)


def last_kernel(half, dense, mixed, ghosts, slope, source, own, other, adjoint, pieces):
    cols = mixed.shape[1]
    state = new_state(dense, mixed, ghosts, source)
    adjoint[...] = state.astype(BF16)
    pre_grad = (slope[...] * state).astype(BF16)
    count = pieces.shape[0] // 2
    sides = cols // 128
    for features, place in ((own, half[0]), (other, 1 - half[0])):
        part = dot(features[...], pre_grad, ((0,), (0,))).astype(BF16)
        for group in range(cols // 8):
            for side in range(sides):
                pieces[place * count + group * sides + side] = part[
                    group * 8:group * 8 + 8, side * 128:side * 128 + 128
                ]


def last(half, dense, mixed, ghosts, slope, source, own, other):
    rows, cols = mixed.shape
    return pl.pallas_call(
        last_kernel,
        out_shape=(
            jax.ShapeDtypeStruct((rows, cols), BF16),
            jax.ShapeDtypeStruct((2 * cols * cols // 1024, 8, 128), BF16),
        ),
        in_specs=[SMEM] + [VMEM] * 7,
        out_specs=(VMEM, VMEM),
        compiler_params=params(24),
        name="last",
    )(half, dense, mixed, ghosts, slope, source, own, other)


def total_kernel(terms_count, scale, terms, spread):
    value = terms[0].astype(F32)
    for term in range(1, terms_count):
        value = value + terms[term].astype(F32)
    value = (value * scale).astype(BF16)
    for copy in range(spread.shape[0]):
        spread[copy] = value


def total(terms, terms_count, copies, scale):
    blocks = terms.shape[0] // terms_count
    out = pl.pallas_call(
        lambda *refs: total_kernel(terms_count, scale, *refs),
        out_shape=jax.ShapeDtypeStruct((copies, blocks) + terms.shape[1:], BF16),
        in_specs=[VMEM],
        out_specs=VMEM,
        compiler_params=params(16),
        name="total",
    )(terms.reshape((terms_count, blocks) + terms.shape[1:]))
    return out.reshape((copies * blocks,) + terms.shape[1:])


def unpack_kernel(pieces, grad, wide, sems):
    sides = grad.shape[1] // 128
    parts = sems.shape[0]
    run = pieces.shape[0] // parts
    lines = grad.shape[0] // parts
    leaves = []
    for part in range(parts):
        for piece in range(part * run, part * run + run):
            group, side = divmod(piece, sides)
            wide[group * 8:group * 8 + 8, side * 128:side * 128 + 128] = pieces[piece].astype(F32)
        here = pl.ds(part * lines, lines)
        leaves.append(pltpu.make_async_copy(wide.at[here], grad.at[here], sems.at[part]))
        leaves[-1].start()
    for leave in leaves:
        leave.wait()


def shards(grad_out, preact, aggregated, weight, tiles, in_block, out_block, tile_count, send_rows):
    rows, cols = grad_out.shape
    peers = lax.axis_size("dom")
    sent = send_rows.shape[1] * send_rows.shape[2]
    half = lax.axis_index("feat")
    half = half.reshape(1)
    other_weight = lax.ppermute(weight, "feat", SWAP)
    pick = choose(send_rows[0].T, rows)
    hyperbolic = jnp.tanh(preact.astype(F32))
    slope = 1.0 - hyperbolic * hyperbolic
    scaled = (slope * grad_out.astype(F32)).astype(BF16)
    for iteration in range(ITERS):
        other = lax.ppermute(scaled, "feat", SWAP)
        mixed, outgoing = mix(half, tile_count, scaled, other, weight, other_weight, pick)
        if iteration == 1:
            outgoing, other_agg = lax.optimization_barrier((outgoing, other_agg))
        ghosts = lax.all_to_all(
            outgoing.reshape(peers, sent // peers, cols), "dom", split_axis=0, concat_axis=0, tiled=True
        ).reshape(sent, cols)
        if iteration == 0:
            scaled, dense = first(
                tile_count, in_block, out_block, tiles, mixed, ghosts, slope, grad_out
            )
            scaled, aggregated = lax.optimization_barrier((scaled, aggregated))
            other_agg = lax.ppermute(aggregated, "feat", SWAP)
        elif iteration < ITERS - 1:
            scaled = sweep(dense, mixed, ghosts, slope, grad_out)
    adjoint, pieces = last(half, dense, mixed, ghosts, slope, grad_out, aggregated, other_agg)
    lines = peers // RING
    across = [[line * RING + place for line in range(lines)] for place in range(RING)]
    along = [[line * RING + place for place in range(RING)] for line in range(lines)]

    def exchange(blocks, groups):
        return lax.all_to_all(
            blocks, "dom", split_axis=0, concat_axis=0, tiled=True, axis_index_groups=groups
        )

    terms = total(exchange(pieces, across), lines, RING, 1.0)
    spread = total(exchange(terms, along), RING, lines, 1.0 / math.sqrt(peers * rows))
    gathered = exchange(spread, across)
    grad_weight = pl.pallas_call(
        unpack_kernel,
        out_shape=jax.ShapeDtypeStruct((2 * cols, cols), F32),
        in_specs=[VMEM],
        out_specs=pl.BlockSpec(memory_space=pl.ANY),
        scratch_shapes=[
            pltpu.VMEM((2 * cols, cols), F32),
            pltpu.SemaphoreType.DMA((4,)),
        ],
        compiler_params=params(16),
        name="unpack",
    )(gathered)
    return adjoint, grad_weight


def solution(mesh):
    placed = (
        P("dom", "feat"),
        P("dom", "feat"),
        P("dom", "feat"),
        P(None, "feat"),
        P("dom", None, None),
        P("dom"),
        P("dom"),
        P("dom"),
        P("dom", None, None),
    )
    return jax.shard_map(
        shards,
        mesh=mesh,
        in_specs=placed,
        out_specs=(P("dom", "feat"), P(None, "feat")),
        check_vma=False,
    )
```

```python
import math

import jax
import jax.numpy as jnp
from jax import lax
from jax.experimental import pallas as pl
from jax.experimental.pallas import tpu as pltpu
from jax.sharding import PartitionSpec as P

ITERS = 3
RING = 8
BF16 = jnp.bfloat16
F32 = jnp.float32
VMEM = pl.BlockSpec(memory_space=pltpu.VMEM)
SMEM = pl.BlockSpec(memory_space=pltpu.SMEM)
SWAP = ((0, 1), (1, 0))


def params(mib):
    return pltpu.CompilerParams(vmem_limit_bytes=mib << 20)


def dot(a, b, dims=((1,), (0,))):
    return lax.dot_general(a, b, (dims, ((), ())), preferred_element_type=F32)


def split(size):
    return slice(0, size // 2), slice(size // 2, size)


def choose_kernel(wanted, pick):
    step, rows = 2 * wanted.shape[0], pick.shape[1]
    row = lax.broadcasted_iota(jnp.int32, (wanted.shape[0], rows), 1)
    for pair in range(wanted.shape[1] // 2):
        parts = [
            (wanted[:, peer:peer + 1] == row).astype(F32) for peer in (2 * pair, 2 * pair + 1)
        ]
        pick[pair * step:pair * step + step, :] = jnp.concatenate(parts, axis=0).astype(BF16)


def choose(wanted, rows):
    return pl.pallas_call(
        choose_kernel,
        out_shape=jax.ShapeDtypeStruct((wanted.shape[0] * wanted.shape[1], rows), BF16),
        in_specs=[VMEM],
        out_specs=VMEM,
        compiler_params=params(16),
        name="choose",
    )(wanted)


def mix_kernel(half, own, other, own_w, other_w, pick, mixed, outgoing):
    cols = own.shape[1]
    mine = pl.ds(pl.multiple_of(half[0] * cols, cols), cols)
    ends = []
    for part in split(own.shape[0]):
        value = dot(own[part, :], own_w[mine, :], ((1,), (1,)))
        value = value + dot(other[part, :], other_w[mine, :], ((1,), (1,)))
        ends.append(value.astype(BF16))
        mixed[part, :] = ends[-1]
    value = jnp.concatenate(ends, axis=0)
    for part in split(pick.shape[0]):
        outgoing[part, :] = dot(pick[part, :], value).astype(BF16)


def mix(half, own, other, own_w, other_w, pick):
    rows, cols = own.shape
    return pl.pallas_call(
        mix_kernel,
        out_shape=(
            jax.ShapeDtypeStruct((rows, cols), BF16),
            jax.ShapeDtypeStruct((pick.shape[0], cols), BF16),
        ),
        in_specs=[SMEM] + [VMEM] * 5,
        out_specs=(VMEM, VMEM),
        compiler_params=params(16),
        cost_estimate=pl.CostEstimate(
            flops=8 * rows * cols * (2 * cols + pick.shape[0]), bytes_accessed=5 << 19, transcendentals=0
        ),
        name="mix",
    )(half, own, other, own_w, other_w, pick)


def new_state(dense, mixed, ghosts, source):
    rows = mixed.shape[0]
    state = dot(dense[:, :rows], mixed[...]) + dot(dense[:, rows:], ghosts[...])
    return state + source[...].astype(F32)


def densify_kernel(count, inputs, outputs, tiles, dense, total):
    size = tiles.shape[1]
    out_blocks = dense.shape[0] // size
    in_blocks = dense.shape[1] // size
    total[...] = jnp.zeros_like(total)

    def step(slot, carry):
        total[outputs[slot] * in_blocks + inputs[slot]] += tiles[slot].astype(F32)
        return carry

    lax.fori_loop(0, count[0], step, 0)
    for out in range(out_blocks):
        for inp in range(in_blocks):
            dense[out * size:(out + 1) * size, inp * size:(inp + 1) * size] = total[
                out * in_blocks + inp
            ].astype(BF16)


def densify(count, inputs, outputs, tiles, rows, across):
    size = tiles.shape[1]
    pairs = rows * across // (size * size)
    return pl.pallas_call(
        densify_kernel,
        out_shape=jax.ShapeDtypeStruct((rows, across), BF16),
        in_specs=[SMEM] * 3 + [VMEM],
        out_specs=VMEM,
        scratch_shapes=[pltpu.VMEM((pairs, size, size), F32)],
        compiler_params=params(8),
        cost_estimate=pl.CostEstimate(flops=1 << 22, bytes_accessed=4 << 20, transcendentals=0),
        name="densify",
    )(count, inputs, outputs, tiles)


def sweep_kernel(dense, mixed, ghosts, slope, source, scaled):
    scaled[...] = (slope[...] * new_state(dense, mixed, ghosts, source)).astype(BF16)


def sweep(dense, mixed, ghosts, slope, source):
    return pl.pallas_call(
        sweep_kernel,
        out_shape=jax.ShapeDtypeStruct(mixed.shape, BF16),
        in_specs=[VMEM] * 5,
        out_specs=VMEM,
        compiler_params=params(16),
        name="sweep",
    )(dense, mixed, ghosts, slope, source)


def last_kernel(half, dense, mixed, ghosts, slope, source, own, other, adjoint, pieces):
    cols = mixed.shape[1]
    state = new_state(dense, mixed, ghosts, source)
    adjoint[...] = state.astype(BF16)
    pre_grad = (slope[...] * state).astype(BF16)
    count = pieces.shape[0] // 2
    sides = cols // 128
    for features, place in ((own, half[0]), (other, 1 - half[0])):
        part = dot(features[...], pre_grad, ((0,), (0,))).astype(BF16)
        for group in range(cols // 8):
            for side in range(sides):
                pieces[place * count + group * sides + side] = part[
                    group * 8:group * 8 + 8, side * 128:side * 128 + 128
                ]


def last(half, dense, mixed, ghosts, slope, source, own, other):
    rows, cols = mixed.shape
    return pl.pallas_call(
        last_kernel,
        out_shape=(
            jax.ShapeDtypeStruct((rows, cols), BF16),
            jax.ShapeDtypeStruct((2 * cols * cols // 1024, 8, 128), BF16),
        ),
        in_specs=[SMEM] + [VMEM] * 7,
        out_specs=(VMEM, VMEM),
        compiler_params=params(24),
        name="last",
    )(half, dense, mixed, ghosts, slope, source, own, other)


def total_kernel(terms_count, scale, terms, spread):
    value = terms[0].astype(F32)
    for term in range(1, terms_count):
        value = value + terms[term].astype(F32)
    value = (value * scale).astype(BF16)
    for copy in range(spread.shape[0]):
        spread[copy] = value


def total(terms, terms_count, copies, scale):
    blocks = terms.shape[0] // terms_count
    out = pl.pallas_call(
        lambda *refs: total_kernel(terms_count, scale, *refs),
        out_shape=jax.ShapeDtypeStruct((copies, blocks) + terms.shape[1:], BF16),
        in_specs=[VMEM],
        out_specs=VMEM,
        compiler_params=params(16),
        name="total",
    )(terms.reshape((terms_count, blocks) + terms.shape[1:]))
    return out.reshape((copies * blocks,) + terms.shape[1:])


def unpack_kernel(pieces, grad, wide, sems):
    sides = grad.shape[1] // 128
    parts = sems.shape[0]
    run = pieces.shape[0] // parts
    lines = grad.shape[0] // parts
    leaves = []
    for part in range(parts):
        for piece in range(part * run, part * run + run):
            group, side = divmod(piece, sides)
            wide[group * 8:group * 8 + 8, side * 128:side * 128 + 128] = pieces[piece].astype(F32)
        here = pl.ds(part * lines, lines)
        leaves.append(pltpu.make_async_copy(wide.at[here], grad.at[here], sems.at[part]))
        leaves[-1].start()
    for leave in leaves:
        leave.wait()


def shards(grad_out, preact, aggregated, weight, tiles, in_block, out_block, tile_count, send_rows):
    rows, cols = grad_out.shape
    peers = lax.axis_size("dom")
    sent = send_rows.shape[1] * send_rows.shape[2]
    half = lax.axis_index("feat")
    half = half.reshape(1)
    other_weight = lax.ppermute(weight, "feat", SWAP)
    pick = choose(send_rows[0].T, rows)
    hyperbolic = jnp.tanh(preact.astype(F32))
    slope = 1.0 - hyperbolic * hyperbolic
    scaled = (slope * grad_out.astype(F32)).astype(BF16)
    for iteration in range(ITERS):
        other = lax.ppermute(scaled, "feat", SWAP)
        mixed, outgoing = mix(half, scaled, other, weight, other_weight, pick)
        if iteration == 1:
            outgoing, other_agg = lax.optimization_barrier((outgoing, other_agg))
        ghosts = lax.all_to_all(
            outgoing.reshape(peers, sent // peers, cols), "dom", split_axis=0, concat_axis=0, tiled=True
        ).reshape(sent, cols)
        if iteration == 0:
            dense = densify(tile_count, in_block, out_block, tiles, rows, rows + sent)
            mixed = pltpu.with_memory_space_constraint(mixed, pltpu.VMEM)
            ghosts = pltpu.with_memory_space_constraint(ghosts, pltpu.VMEM)
            scaled = sweep(dense, mixed, ghosts, slope, grad_out)
            scaled, aggregated = lax.optimization_barrier((scaled, aggregated))
            other_agg = lax.ppermute(aggregated, "feat", SWAP)
        elif iteration < ITERS - 1:
            scaled = sweep(dense, mixed, ghosts, slope, grad_out)
    adjoint, pieces = last(half, dense, mixed, ghosts, slope, grad_out, aggregated, other_agg)
    lines = peers // RING
    across = [[line * RING + place for line in range(lines)] for place in range(RING)]
    along = [[line * RING + place for place in range(RING)] for line in range(lines)]

    def exchange(blocks, groups):
        return lax.all_to_all(
            blocks, "dom", split_axis=0, concat_axis=0, tiled=True, axis_index_groups=groups
        )

    terms = total(exchange(pieces, across), lines, RING, 1.0)
    spread = total(exchange(terms, along), RING, lines, 1.0 / math.sqrt(peers * rows))
    gathered = exchange(spread, across)
    grad_weight = pl.pallas_call(
        unpack_kernel,
        out_shape=jax.ShapeDtypeStruct((2 * cols, cols), F32),
        in_specs=[VMEM],
        out_specs=pl.BlockSpec(memory_space=pl.ANY),
        scratch_shapes=[
            pltpu.VMEM((2 * cols, cols), F32),
            pltpu.SemaphoreType.DMA((4,)),
        ],
        compiler_params=params(16),
        name="unpack",
    )(gathered)
    return adjoint, grad_weight


def solution(mesh):
    placed = (
        P("dom", "feat"),
        P("dom", "feat"),
        P("dom", "feat"),
        P(None, "feat"),
        P("dom", None, None),
        P("dom"),
        P("dom"),
        P("dom"),
        P("dom", None, None),
    )
    return jax.shard_map(
        shards,
        mesh=mesh,
        in_specs=placed,
        out_specs=(P("dom", "feat"), P(None, "feat")),
        check_vma=False,
    )
```

```python
import math

import jax
import jax.numpy as jnp
from jax import lax
from jax.experimental import pallas as pl
from jax.experimental.pallas import tpu as pltpu
from jax.sharding import PartitionSpec as P

ITERS = 3
RING = 8
BF16 = jnp.bfloat16
F32 = jnp.float32
VMEM = pl.BlockSpec(memory_space=pltpu.VMEM)
SMEM = pl.BlockSpec(memory_space=pltpu.SMEM)
SWAP = ((0, 1), (1, 0))


def params(mib):
    return pltpu.CompilerParams(vmem_limit_bytes=mib << 20)


def dot(a, b, dims=((1,), (0,))):
    return lax.dot_general(a, b, (dims, ((), ())), preferred_element_type=F32)


def split(size):
    return slice(0, size // 2), slice(size // 2, size)


def choose_kernel(wanted, pick):
    step, rows = 2 * wanted.shape[0], pick.shape[1]
    row = lax.broadcasted_iota(jnp.int32, (wanted.shape[0], rows), 1)
    for pair in range(wanted.shape[1] // 2):
        parts = [
            (wanted[:, peer:peer + 1] == row).astype(F32) for peer in (2 * pair, 2 * pair + 1)
        ]
        pick[pair * step:pair * step + step, :] = jnp.concatenate(parts, axis=0).astype(BF16)


def choose(wanted, rows):
    return pl.pallas_call(
        choose_kernel,
        out_shape=jax.ShapeDtypeStruct((wanted.shape[0] * wanted.shape[1], rows), BF16),
        in_specs=[VMEM],
        out_specs=VMEM,
        compiler_params=params(16),
        name="choose",
    )(wanted)


def mix_kernel(half, own, other, own_w, other_w, pick, mixed, outgoing, *stage):
    cols = own.shape[1]
    mine = pl.ds(pl.multiple_of(half[0] * cols, cols), cols)
    ends = []
    for part in split(own.shape[0]):
        value = dot(own[part, :], own_w[mine, :], ((1,), (1,)))
        value = value + dot(other[part, :], other_w[mine, :], ((1,), (1,)))
        ends.append(value.astype(BF16))
        mixed[part, :] = ends[-1]
    value = jnp.concatenate(ends, axis=0)
    if not stage:
        for part in split(pick.shape[0]):
            outgoing[part, :] = dot(pick[part, :], value).astype(BF16)
        return
    staged, sems = stage
    run = pick.shape[0] // sems.shape[0]
    leaves = []
    for index in range(sems.shape[0]):
        here = pl.ds(index * run, run)
        staged[here, :] = dot(pick[here, :], value).astype(BF16)
        leaves.append(pltpu.make_async_copy(staged.at[here], outgoing.at[here], sems.at[index]))
        leaves[-1].start()
    for leave in leaves:
        leave.wait()


def mix(half, own, other, own_w, other_w, pick, away):
    rows, cols = own.shape
    sent = pick.shape[0]
    return pl.pallas_call(
        mix_kernel,
        out_shape=(
            jax.ShapeDtypeStruct((rows, cols), BF16),
            jax.ShapeDtypeStruct((pick.shape[0], cols), BF16),
        ),
        in_specs=[SMEM] + [VMEM] * 5,
        out_specs=(VMEM, pl.BlockSpec(memory_space=pl.ANY) if away else VMEM),
        scratch_shapes=[
            pltpu.VMEM((sent, cols), BF16),
            pltpu.SemaphoreType.DMA((4,)),
        ] if away else [],
        compiler_params=params(16),
        cost_estimate=pl.CostEstimate(
            flops=8 * rows * cols * (2 * cols + pick.shape[0]), bytes_accessed=5 << 19, transcendentals=0
        ),
        name="mix",
    )(half, own, other, own_w, other_w, pick)


def new_state(dense, mixed, ghosts, source):
    rows = mixed.shape[0]
    state = dot(dense[:, :rows], mixed[...]) + dot(dense[:, rows:], ghosts[...])
    return state + source[...].astype(F32)


def densify_kernel(count, inputs, outputs, tiles, dense, total):
    size = tiles.shape[1]
    out_blocks = dense.shape[0] // size
    in_blocks = dense.shape[1] // size
    total[...] = jnp.zeros_like(total)

    def step(slot, carry):
        total[outputs[slot] * in_blocks + inputs[slot]] += tiles[slot].astype(F32)
        return carry

    lax.fori_loop(0, count[0], step, 0)
    for out in range(out_blocks):
        for inp in range(in_blocks):
            dense[out * size:(out + 1) * size, inp * size:(inp + 1) * size] = total[
                out * in_blocks + inp
            ].astype(BF16)


def densify(count, inputs, outputs, tiles, rows, across):
    size = tiles.shape[1]
    pairs = rows * across // (size * size)
    return pl.pallas_call(
        densify_kernel,
        out_shape=jax.ShapeDtypeStruct((rows, across), BF16),
        in_specs=[SMEM] * 3 + [VMEM],
        out_specs=VMEM,
        scratch_shapes=[pltpu.VMEM((pairs, size, size), F32)],
        compiler_params=params(8),
        cost_estimate=pl.CostEstimate(flops=1 << 22, bytes_accessed=4 << 20, transcendentals=0),
        name="densify",
    )(count, inputs, outputs, tiles)


def sweep_kernel(dense, mixed, ghosts, slope, source, scaled):
    scaled[...] = (slope[...] * new_state(dense, mixed, ghosts, source)).astype(BF16)


def sweep(dense, mixed, ghosts, slope, source):
    return pl.pallas_call(
        sweep_kernel,
        out_shape=jax.ShapeDtypeStruct(mixed.shape, BF16),
        in_specs=[VMEM] * 5,
        out_specs=VMEM,
        compiler_params=params(16),
        name="sweep",
    )(dense, mixed, ghosts, slope, source)


def last_kernel(half, dense, mixed, ghosts, slope, source, own, other, adjoint, pieces):
    cols = mixed.shape[1]
    state = new_state(dense, mixed, ghosts, source)
    adjoint[...] = state.astype(BF16)
    pre_grad = (slope[...] * state).astype(BF16)
    count = pieces.shape[0] // 2
    sides = cols // 128
    for features, place in ((own, half[0]), (other, 1 - half[0])):
        part = dot(features[...], pre_grad, ((0,), (0,))).astype(BF16)
        for group in range(cols // 8):
            for side in range(sides):
                pieces[place * count + group * sides + side] = part[
                    group * 8:group * 8 + 8, side * 128:side * 128 + 128
                ]


def last(half, dense, mixed, ghosts, slope, source, own, other):
    rows, cols = mixed.shape
    return pl.pallas_call(
        last_kernel,
        out_shape=(
            jax.ShapeDtypeStruct((rows, cols), BF16),
            jax.ShapeDtypeStruct((2 * cols * cols // 1024, 8, 128), BF16),
        ),
        in_specs=[SMEM] + [VMEM] * 7,
        out_specs=(VMEM, VMEM),
        compiler_params=params(24),
        name="last",
    )(half, dense, mixed, ghosts, slope, source, own, other)


def total_kernel(terms_count, scale, terms, spread):
    value = terms[0].astype(F32)
    for term in range(1, terms_count):
        value = value + terms[term].astype(F32)
    value = (value * scale).astype(BF16)
    for copy in range(spread.shape[0]):
        spread[copy] = value


def total(terms, terms_count, copies, scale):
    blocks = terms.shape[0] // terms_count
    out = pl.pallas_call(
        lambda *refs: total_kernel(terms_count, scale, *refs),
        out_shape=jax.ShapeDtypeStruct((copies, blocks) + terms.shape[1:], BF16),
        in_specs=[VMEM],
        out_specs=VMEM,
        compiler_params=params(16),
        name="total",
    )(terms.reshape((terms_count, blocks) + terms.shape[1:]))
    return out.reshape((copies * blocks,) + terms.shape[1:])


def unpack_kernel(pieces, grad, wide, sems):
    sides = grad.shape[1] // 128
    parts = sems.shape[0]
    run = pieces.shape[0] // parts
    lines = grad.shape[0] // parts
    leaves = []
    for part in range(parts):
        for piece in range(part * run, part * run + run):
            group, side = divmod(piece, sides)
            wide[group * 8:group * 8 + 8, side * 128:side * 128 + 128] = pieces[piece].astype(F32)
        here = pl.ds(part * lines, lines)
        leaves.append(pltpu.make_async_copy(wide.at[here], grad.at[here], sems.at[part]))
        leaves[-1].start()
    for leave in leaves:
        leave.wait()


def shards(grad_out, preact, aggregated, weight, tiles, in_block, out_block, tile_count, send_rows):
    rows, cols = grad_out.shape
    peers = lax.axis_size("dom")
    sent = send_rows.shape[1] * send_rows.shape[2]
    half = lax.axis_index("feat")
    half = half.reshape(1)
    other_weight = lax.ppermute(weight, "feat", SWAP)
    pick = choose(send_rows[0].T, rows)
    hyperbolic = jnp.tanh(preact.astype(F32))
    slope = 1.0 - hyperbolic * hyperbolic
    scaled = (slope * grad_out.astype(F32)).astype(BF16)
    for iteration in range(ITERS):
        other = lax.ppermute(scaled, "feat", SWAP)
        mixed, outgoing = mix(half, scaled, other, weight, other_weight, pick, iteration == 0)
        if iteration == 1:
            outgoing, other_agg = lax.optimization_barrier((outgoing, other_agg))
        ghosts = lax.all_to_all(
            outgoing.reshape(peers, sent // peers, cols), "dom", split_axis=0, concat_axis=0, tiled=True
        ).reshape(sent, cols)
        if iteration == 0:
            dense = densify(tile_count, in_block, out_block, tiles, rows, rows + sent)
            mixed = pltpu.with_memory_space_constraint(mixed, pltpu.VMEM)
            ghosts = pltpu.with_memory_space_constraint(ghosts, pltpu.VMEM)
            scaled = sweep(dense, mixed, ghosts, slope, grad_out)
            scaled, aggregated = lax.optimization_barrier((scaled, aggregated))
            other_agg = lax.ppermute(aggregated, "feat", SWAP)
        elif iteration < ITERS - 1:
            scaled = sweep(dense, mixed, ghosts, slope, grad_out)
    adjoint, pieces = last(half, dense, mixed, ghosts, slope, grad_out, aggregated, other_agg)
    lines = peers // RING
    across = [[line * RING + place for line in range(lines)] for place in range(RING)]
    along = [[line * RING + place for place in range(RING)] for line in range(lines)]

    def exchange(blocks, groups):
        return lax.all_to_all(
            blocks, "dom", split_axis=0, concat_axis=0, tiled=True, axis_index_groups=groups
        )

    terms = total(exchange(pieces, across), lines, RING, 1.0)
    spread = total(exchange(terms, along), RING, lines, 1.0 / math.sqrt(peers * rows))
    gathered = exchange(spread, across)
    grad_weight = pl.pallas_call(
        unpack_kernel,
        out_shape=jax.ShapeDtypeStruct((2 * cols, cols), F32),
        in_specs=[VMEM],
        out_specs=pl.BlockSpec(memory_space=pl.ANY),
        scratch_shapes=[
            pltpu.VMEM((2 * cols, cols), F32),
            pltpu.SemaphoreType.DMA((4,)),
        ],
        compiler_params=params(16),
        name="unpack",
    )(gathered)
    return adjoint, grad_weight


def solution(mesh):
    placed = (
        P("dom", "feat"),
        P("dom", "feat"),
        P("dom", "feat"),
        P(None, "feat"),
        P("dom", None, None),
        P("dom"),
        P("dom"),
        P("dom"),
        P("dom", None, None),
    )
    return jax.shard_map(
        shards,
        mesh=mesh,
        in_specs=placed,
        out_specs=(P("dom", "feat"), P(None, "feat")),
        check_vma=False,
    )
```

```python
import math

import jax
import jax.numpy as jnp
from jax import lax
from jax.experimental import pallas as pl
from jax.experimental.pallas import tpu as pltpu
from jax.sharding import PartitionSpec as P

ITERS = 3
RING = 8
BF16 = jnp.bfloat16
F32 = jnp.float32
VMEM = pl.BlockSpec(memory_space=pltpu.VMEM)
SMEM = pl.BlockSpec(memory_space=pltpu.SMEM)
SWAP = ((0, 1), (1, 0))


def params(mib):
    return pltpu.CompilerParams(vmem_limit_bytes=mib << 20)


def dot(a, b, dims=((1,), (0,))):
    return lax.dot_general(a, b, (dims, ((), ())), preferred_element_type=F32)


def split(size):
    return slice(0, size // 2), slice(size // 2, size)


def choose_kernel(wanted, pick):
    step, rows = 2 * wanted.shape[0], pick.shape[1]
    row = lax.broadcasted_iota(jnp.int32, (wanted.shape[0], rows), 1)
    for pair in range(wanted.shape[1] // 2):
        parts = [
            (wanted[:, peer:peer + 1] == row).astype(F32) for peer in (2 * pair, 2 * pair + 1)
        ]
        pick[pair * step:pair * step + step, :] = jnp.concatenate(parts, axis=0).astype(BF16)


def choose(wanted, rows):
    return pl.pallas_call(
        choose_kernel,
        out_shape=jax.ShapeDtypeStruct((wanted.shape[0] * wanted.shape[1], rows), BF16),
        in_specs=[VMEM],
        out_specs=VMEM,
        compiler_params=params(16),
        name="choose",
    )(wanted)


def mix_kernel(half, own, other, own_w, other_w, pick, mixed, outgoing):
    cols = own.shape[1]
    mine = pl.ds(pl.multiple_of(half[0] * cols, cols), cols)
    ends = []
    for part in split(own.shape[0]):
        value = dot(own[part, :], own_w[mine, :], ((1,), (1,)))
        value = value + dot(other[part, :], other_w[mine, :], ((1,), (1,)))
        ends.append(value.astype(BF16))
        mixed[part, :] = ends[-1]
    value = jnp.concatenate(ends, axis=0)
    for part in split(pick.shape[0]):
        outgoing[part, :] = dot(pick[part, :], value).astype(BF16)


def mix(half, own, other, own_w, other_w, pick):
    rows, cols = own.shape
    return pl.pallas_call(
        mix_kernel,
        out_shape=(
            jax.ShapeDtypeStruct((rows, cols), BF16),
            jax.ShapeDtypeStruct((pick.shape[0], cols), BF16),
        ),
        in_specs=[SMEM] + [VMEM] * 5,
        out_specs=(VMEM, VMEM),
        compiler_params=params(16),
        cost_estimate=pl.CostEstimate(
            flops=8 * rows * cols * (2 * cols + pick.shape[0]), bytes_accessed=5 << 19, transcendentals=0
        ),
        name="mix",
    )(half, own, other, own_w, other_w, pick)


def new_state(dense, mixed, ghosts, source):
    rows = mixed.shape[0]
    state = dot(dense[:, :rows], mixed[...]) + dot(dense[:, rows:], ghosts[...])
    return state + source[...].astype(F32)


def densify_kernel(count, inputs, outputs, tiles, dense, total):
    size = tiles.shape[1]
    out_blocks = dense.shape[0] // size
    in_blocks = dense.shape[1] // size
    total[...] = jnp.zeros_like(total)

    def step(slot, carry):
        total[outputs[slot] * in_blocks + inputs[slot]] += tiles[slot].astype(F32)
        return carry

    lax.fori_loop(0, count[0], step, 0)
    for out in range(out_blocks):
        for inp in range(in_blocks):
            dense[out * size:(out + 1) * size, inp * size:(inp + 1) * size] = total[
                out * in_blocks + inp
            ].astype(BF16)


def densify(count, inputs, outputs, tiles, rows, across):
    size = tiles.shape[1]
    pairs = rows * across // (size * size)
    return pl.pallas_call(
        densify_kernel,
        out_shape=jax.ShapeDtypeStruct((rows, across), BF16),
        in_specs=[SMEM] * 3 + [VMEM],
        out_specs=VMEM,
        scratch_shapes=[pltpu.VMEM((pairs, size, size), F32)],
        compiler_params=params(8),
        cost_estimate=pl.CostEstimate(flops=1 << 22, bytes_accessed=4 << 20, transcendentals=0),
        name="densify",
    )(count, inputs, outputs, tiles)


def sweep_kernel(dense, mixed, ghosts, slope, source, scaled):
    scaled[...] = (slope[...] * new_state(dense, mixed, ghosts, source)).astype(BF16)


def sweep(dense, mixed, ghosts, slope, source):
    return pl.pallas_call(
        sweep_kernel,
        out_shape=jax.ShapeDtypeStruct(mixed.shape, BF16),
        in_specs=[VMEM] * 5,
        out_specs=VMEM,
        compiler_params=params(16),
        name="sweep",
    )(dense, mixed, ghosts, slope, source)


def last_kernel(half, dense, mixed, ghosts, slope, source, own, other, adjoint, pieces):
    cols = mixed.shape[1]
    state = new_state(dense, mixed, ghosts, source)
    adjoint[...] = state.astype(BF16)
    pre_grad = (slope[...] * state).astype(BF16)
    count = pieces.shape[0] // 2
    sides = cols // 128
    for features, place in ((own, half[0]), (other, 1 - half[0])):
        part = dot(features[...], pre_grad, ((0,), (0,))).astype(BF16)
        for group in range(cols // 8):
            for side in range(sides):
                pieces[place * count + group * sides + side] = part[
                    group * 8:group * 8 + 8, side * 128:side * 128 + 128
                ]


def last(half, dense, mixed, ghosts, slope, source, own, other):
    rows, cols = mixed.shape
    return pl.pallas_call(
        last_kernel,
        out_shape=(
            jax.ShapeDtypeStruct((rows, cols), BF16),
            jax.ShapeDtypeStruct((2 * cols * cols // 1024, 8, 128), BF16),
        ),
        in_specs=[SMEM] + [VMEM] * 7,
        out_specs=(VMEM, VMEM),
        compiler_params=params(24),
        name="last",
    )(half, dense, mixed, ghosts, slope, source, own, other)


def total_kernel(terms_count, scale, terms, spread):
    value = terms[0].astype(F32)
    for term in range(1, terms_count):
        value = value + terms[term].astype(F32)
    value = (value * scale).astype(BF16)
    for copy in range(spread.shape[0]):
        spread[copy] = value


def total(terms, terms_count, copies, scale):
    blocks = terms.shape[0] // terms_count
    out = pl.pallas_call(
        lambda *refs: total_kernel(terms_count, scale, *refs),
        out_shape=jax.ShapeDtypeStruct((copies, blocks) + terms.shape[1:], BF16),
        in_specs=[VMEM],
        out_specs=VMEM,
        compiler_params=params(16),
        name="total",
    )(terms.reshape((terms_count, blocks) + terms.shape[1:]))
    return out.reshape((copies * blocks,) + terms.shape[1:])


def unpack_kernel(pieces, grad, wide, sems):
    sides = grad.shape[1] // 128
    parts = sems.shape[0]
    run = pieces.shape[0] // parts
    lines = grad.shape[0] // parts
    leaves = []
    for part in range(parts):
        for piece in range(part * run, part * run + run):
            group, side = divmod(piece, sides)
            wide[group * 8:group * 8 + 8, side * 128:side * 128 + 128] = pieces[piece].astype(F32)
        here = pl.ds(part * lines, lines)
        leaves.append(pltpu.make_async_copy(wide.at[here], grad.at[here], sems.at[part]))
        leaves[-1].start()
    for leave in leaves:
        leave.wait()


def shards(grad_out, preact, aggregated, weight, tiles, in_block, out_block, tile_count, send_rows):
    rows, cols = grad_out.shape
    peers = lax.axis_size("dom")
    sent = send_rows.shape[1] * send_rows.shape[2]
    half = lax.axis_index("feat")
    half = half.reshape(1)
    other_weight = lax.ppermute(weight, "feat", SWAP)
    wanted = send_rows[0].T
    pick = choose(wanted, rows)
    hyperbolic = jnp.tanh(preact.astype(F32))
    slope = 1.0 - hyperbolic * hyperbolic
    scaled = (slope * grad_out.astype(F32)).astype(BF16)
    for iteration in range(ITERS):
        other = lax.ppermute(scaled, "feat", SWAP)
        mixed, outgoing = mix(half, scaled, other, weight, other_weight, pick)
        if iteration == 1:
            outgoing, other_agg = lax.optimization_barrier((outgoing, other_agg))
        if iteration == 0:
            outgoing, again = lax.optimization_barrier((outgoing, wanted))
        ghosts = lax.all_to_all(
            outgoing.reshape(peers, sent // peers, cols), "dom", split_axis=0, concat_axis=0, tiled=True
        ).reshape(sent, cols)
        if iteration == 0:
            pick = choose(again, rows)
            dense = densify(tile_count, in_block, out_block, tiles, rows, rows + sent)
            mixed = pltpu.with_memory_space_constraint(mixed, pltpu.VMEM)
            ghosts = pltpu.with_memory_space_constraint(ghosts, pltpu.VMEM)
            scaled = sweep(dense, mixed, ghosts, slope, grad_out)
            scaled, aggregated = lax.optimization_barrier((scaled, aggregated))
            other_agg = lax.ppermute(aggregated, "feat", SWAP)
        elif iteration < ITERS - 1:
            scaled = sweep(dense, mixed, ghosts, slope, grad_out)
    adjoint, pieces = last(half, dense, mixed, ghosts, slope, grad_out, aggregated, other_agg)
    lines = peers // RING
    across = [[line * RING + place for line in range(lines)] for place in range(RING)]
    along = [[line * RING + place for place in range(RING)] for line in range(lines)]

    def exchange(blocks, groups):
        return lax.all_to_all(
            blocks, "dom", split_axis=0, concat_axis=0, tiled=True, axis_index_groups=groups
        )

    terms = total(exchange(pieces, across), lines, RING, 1.0)
    spread = total(exchange(terms, along), RING, lines, 1.0 / math.sqrt(peers * rows))
    gathered = exchange(spread, across)
    grad_weight = pl.pallas_call(
        unpack_kernel,
        out_shape=jax.ShapeDtypeStruct((2 * cols, cols), F32),
        in_specs=[VMEM],
        out_specs=pl.BlockSpec(memory_space=pl.ANY),
        scratch_shapes=[
            pltpu.VMEM((2 * cols, cols), F32),
            pltpu.SemaphoreType.DMA((4,)),
        ],
        compiler_params=params(16),
        name="unpack",
    )(gathered)
    return adjoint, grad_weight


def solution(mesh):
    placed = (
        P("dom", "feat"),
        P("dom", "feat"),
        P("dom", "feat"),
        P(None, "feat"),
        P("dom", None, None),
        P("dom"),
        P("dom"),
        P("dom"),
        P("dom", None, None),
    )
    return jax.shard_map(
        shards,
        mesh=mesh,
        in_specs=placed,
        out_specs=(P("dom", "feat"), P(None, "feat")),
        check_vma=False,
    )
```
